256 devices in a mesh: dp: 32 (over x_hi, z, core), section: 8 (over y, x_lo).
Axes of the slice: x: 4 (x_hi: 2, x_lo: 2; x = x_hi * 2 + x_lo), y: 4, z: 8, core: 2. Of those that a mesh axis runs over, the one named last changes fastest.
Arguments:
- features: bfloat16 [64, 16, 5120], P('dp'), may hold values from -6 to 6
- target: bfloat16 [64, 16, 5120], P('dp'), may hold values from -6 to 6
- timesteps: int32 [64], P('dp'), may hold values from 0 to 999
- conv_one: bfloat16 [8, 2880, 320], P('section'), may hold values from -0.109375 to 0.109375
- conv_two: bfloat16 [8, 2880, 320], P('section'), may hold values from -0.109375 to 0.109375
- time_proj: float32 [8, 320, 320], P('section'), may hold values from -0.3125 to 0.3125
Outputs:
- grad_one: float32 [8, 2880, 320], P('section')
- grad_two: float32 [8, 2880, 320], P('section')
- grad_time: float32 [8, 320, 320], P('section')
The draws below stay inside these ranges and needn't reach their ends.
All inputs are finite; a program needn't handle non-finite values.
Results may differ from the reference program's by a relative error of at most 0.002.
Values sent between devices are 32-bit elements; how exact they have to be, the bound alone decides.
No kernel may reach another device: no remote copies, remote signals or barrier semaphores. Data moves between devices by JAX's collectives and lax.ppermute only.
A program may use at most 128 MiB of HBM per device.

```python
import math
import jax
import jax.numpy as jnp
from jax import lax

CH = 320
TE = 320
GROUPS = 32
HEIGHT = 16
WIDTH = 16
BATCH = 64
KROWS = 2880
SECTIONS = 8
N_SECTION = 8


def place_ends(drawn, own_key, low, largest):
    place = [jax.random.randint(jax.random.fold_in(own_key, axis), (), 0, length) for axis, length in enumerate(drawn.shape)]
    widest = drawn.shape.index(max(drawn.shape))
    next_to = place[:widest] + [(place[widest] + 1) % drawn.shape[widest]] + place[widest + 1:]
    return drawn.at[tuple(place)].set(low).at[tuple(next_to)].set(largest)


def steps_of(rng, extent, split, least, high):
    level = 1.0
    for position, parts in split:
        heights = jax.random.uniform(jax.random.fold_in(jax.random.fold_in(rng, 6), position), (parts,), jnp.float32, least / len(split), high / len(split))
        level = level * jnp.repeat(jnp.exp(heights), extent[position] // parts).reshape((-1,) + (1,) * (len(extent) - 1 - position))
    return level


def normal_values(own_key, extent, scale, limit, shards=(), kind=jnp.bfloat16):
    factor_of = steps_of(own_key, extent, shards, -0.22, 0.18) if shards else 1.0
    drawn = jax.random.normal(own_key, extent, jnp.float32) * scale * factor_of
    return jnp.minimum(jnp.maximum(drawn, -limit), limit).astype(kind)


def setup_inputs(seed: int = 0) -> dict:
    streams_of = jax.random.split(jax.random.key(seed), 7)
    return {
        "features": normal_values(streams_of[0], (BATCH, HEIGHT, WIDTH * CH), 1.0, 6.0, ((0, 32),)),
        "target": normal_values(streams_of[1], (BATCH, HEIGHT, WIDTH * CH), 1.0, 6.0, ((0, 32),)),
        "timesteps": place_ends(jax.random.randint(streams_of[2], (BATCH,), 0, 1000), jax.random.fold_in(streams_of[2], 1), 0, 999).astype(jnp.int32),
        "conv_one": normal_values(streams_of[3], (SECTIONS, KROWS, CH), KROWS ** -0.5, 0.109375, ((0, 8),)),
        "conv_two": normal_values(streams_of[4], (SECTIONS, KROWS, CH), KROWS ** -0.5, 0.109375, ((0, 8),)),
        "time_proj": normal_values(streams_of[5], (SECTIONS, TE, CH), TE ** -0.5, 0.3125, ((0, 8),), jnp.float32),
    }


def embed_times(times):
    middle = TE // 2
    freqs = jnp.exp(-math.log(10000.0) * jnp.arange(middle, dtype=jnp.float32) / middle)
    angles = times.astype(jnp.float32)[:, None] * freqs[None, :]
    return jnp.concatenate([jnp.cos(angles), jnp.sin(angles)], axis=1)

def norm_silu(values):
    count, height, width, chans = values.shape
    grouped = values.reshape(count, height, width, GROUPS, chans // GROUPS)
    center = lax.optimization_barrier(jnp.mean(grouped, axis=(1, 2, 4), keepdims=True))
    spread = lax.optimization_barrier(jnp.mean(jnp.square(grouped - center), axis=(1, 2, 4), keepdims=True))
    normed = ((grouped - center) * lax.rsqrt(spread + 1e-05)).reshape(values.shape)
    return jax.nn.silu(normed)

def patches(acts):
    height, width = (acts.shape[1], acts.shape[2])
    padded = jnp.pad(acts, ((0, 0), (1, 1), (1, 1), (0, 0)))
    taps = [padded[:, row_shift:row_shift + height, col_shift:col_shift + width, :] for row_shift in range(3) for col_shift in range(3)]
    return jnp.concatenate(taps, axis=-1)

def conv_apply(acts, weights):
    cols = patches(acts)
    flat = cols.reshape(-1, cols.shape[-1])
    result = jnp.dot(flat, weights, preferred_element_type=jnp.float32)
    return result.reshape(acts.shape[:3] + (weights.shape[1],))

def conv_back(grads, weights):
    count, height, width, chans = grads.shape
    flat = grads.reshape(-1, chans)
    spread_back = jnp.dot(flat, weights.T, preferred_element_type=jnp.float32)
    in_chans = weights.shape[0] // 9
    spread_back = spread_back.reshape(count, height, width, 9, in_chans)
    padded = jnp.zeros((count, height + 2, width + 2, in_chans), jnp.float32)
    for index in range(9):
        row_shift, col_shift = (index // 3, index % 3)
        padded = padded.at[:, row_shift:row_shift + height, col_shift:col_shift + width, :].add(spread_back[:, :, :, index, :])
    return padded[:, 1:-1, 1:-1, :]

def weight_grad(acts, grads):
    cols = patches(acts)
    flat = cols.reshape(-1, cols.shape[-1])
    return lax.dot_general(flat, grads.reshape(-1, grads.shape[-1]), (((0,), (0,)), ((), ())), preferred_element_type=jnp.float32)

def section_forward(section_in, bias_rows, weight_one, weight_two):
    acts_one = norm_silu(section_in).astype(jnp.bfloat16)
    conv_mid = conv_apply(acts_one, weight_one) + bias_rows[:, None, None, :]
    acts_two = norm_silu(conv_mid).astype(jnp.bfloat16)
    return section_in + conv_apply(acts_two, weight_two)

def section_backward(section_in, bias_rows, weight_one, weight_two, grad_out):
    acts_one = norm_silu(section_in).astype(jnp.bfloat16)
    conv_mid = conv_apply(acts_one, weight_one) + bias_rows[:, None, None, :]
    acts_two = norm_silu(conv_mid).astype(jnp.bfloat16)
    grad_low = grad_out.astype(jnp.bfloat16)
    delta_two = weight_grad(acts_two, grad_low)
    grad_acts_two = conv_back(grad_low, weight_two)
    grad_mid = jax.vjp(norm_silu, conv_mid)[1](grad_acts_two)[0]
    grad_bias = lax.optimization_barrier(jnp.sum(grad_mid, axis=(1, 2)))
    grad_mid_low = grad_mid.astype(jnp.bfloat16)
    delta_one = weight_grad(acts_one, grad_mid_low)
    grad_acts_one = conv_back(grad_mid_low, weight_one)
    grad_in = grad_out + jax.vjp(norm_silu, section_in)[1](grad_acts_one)[0]
    return (grad_in, delta_one, delta_two, grad_bias)

def reference(features, target, timesteps, conv_one, conv_two, time_proj):
    batch = features.shape[0]
    middle = N_SECTION // 2
    embedded = embed_times(timesteps)
    current = features.reshape(batch, HEIGHT, WIDTH, CH).astype(jnp.float32)
    inputs_kept = []
    outputs_kept = []
    biases_kept = []
    for section in range(N_SECTION):
        bias_rows = jnp.dot(embedded, time_proj[section], precision=lax.Precision.HIGHEST)
        section_in = current
        if section >= middle:
            section_in = section_in + outputs_kept[N_SECTION - 1 - section]
        result = section_forward(section_in, bias_rows, conv_one[section], conv_two[section])
        inputs_kept.append(section_in)
        outputs_kept.append(result)
        biases_kept.append(bias_rows)
        current = result
    scale = 1.0 / math.sqrt(HEIGHT * WIDTH)
    target_img = target.reshape(batch, HEIGHT, WIDTH, CH)
    grad_next = (current - target_img.astype(jnp.float32)) * scale
    skip_grads = {}
    ones = [None] * N_SECTION
    twos = [None] * N_SECTION
    times_out = [None] * N_SECTION
    for section in range(N_SECTION - 1, -1, -1):
        grad_out = grad_next
        if section < middle:
            grad_out = grad_out + skip_grads[section]
        grad_in, delta_one, delta_two, grad_bias = section_backward(inputs_kept[section], biases_kept[section], conv_one[section], conv_two[section], grad_out)
        ones[section] = delta_one
        twos[section] = delta_two
        times_out[section] = jnp.dot(embedded.T, grad_bias, precision=lax.Precision.HIGHEST)
        grad_next = grad_in
        if section >= middle:
            skip_grads[N_SECTION - 1 - section] = grad_next
    return (jnp.stack(ones), jnp.stack(twos), jnp.stack(times_out))
```

```python
import functools
import math

import jax
import jax.numpy as jnp
from jax import lax
from jax.experimental import pallas as pl
from jax.experimental.pallas import tpu as pltpu
from jax.sharding import Mesh
from jax.sharding import PartitionSpec as P

CH = 320
TE = 320
GROUPS = 32
HEIGHT = 16
WIDTH = 16
PIX = HEIGHT * WIDTH
KROWS = 9 * CH
MICRO = 2
PACK = PIX * CH // 128
GROWS = KROWS * CH // 128
TROWS = TE * CH // 128
TOTAL = 15360
F32 = jnp.float32
BF16 = jnp.bfloat16
ANY = pl.BlockSpec(memory_space=pl.ANY)
SMEM = pl.BlockSpec(memory_space=pltpu.SMEM)


def unpack(ref):
    tail = ref[2 * PIX : PACK, :]
    last = jnp.concatenate([tail[:, :64], tail[:, 64:]], axis=0)
    return jnp.concatenate([ref[0:PIX, :], ref[PIX : 2 * PIX, :], last], axis=1)


def pack(ref, value):
    ref[0:PIX, :] = value[:, 0:128]
    ref[PIX : 2 * PIX, :] = value[:, 128:256]
    half = PIX // 2
    ref[2 * PIX : PACK, :] = jnp.concatenate([value[:half, 256:320], value[half:, 256:320]], axis=1)


def split3(row):
    high = row.astype(BF16).astype(F32)
    rest = row - high
    mid = rest.astype(BF16).astype(F32)
    return [high, mid, rest - mid]


def group_mean(rows, ones):
    parts = []
    for row in rows:
        parts += split3(row)
    parts += [jnp.zeros_like(rows[0])] * (8 - len(parts))
    sums = jnp.dot(jnp.concatenate(parts, axis=0).astype(BF16), ones, preferred_element_type=F32)
    scale = 1.0 / (PIX * (CH // GROUPS))
    return [(sums[3 * i : 3 * i + 1] + sums[3 * i + 1 : 3 * i + 2] + sums[3 * i + 2 : 3 * i + 3]) * scale for i in range(len(rows))]


def colsum(value):
    return jnp.sum(value, axis=0, keepdims=True)


def normed(value, ones):
    (center,) = group_mean([colsum(value)], ones)
    value = value - center
    (spread,) = group_mean([colsum(value * value)], ones)
    scale = lax.rsqrt(spread + 1e-05)
    return value * scale, scale


def sigmoid(z):
    return 1.0 / (1.0 + jnp.exp(-z))


def norm_back(z, scale, cot, ones):
    gate = sigmoid(z)
    cot = cot * (gate * (1.0 + z * (1.0 - gate)))
    mean_one, mean_two = group_mean([colsum(cot), colsum(cot * z)], ones)
    return scale * (cot - mean_one - z * mean_two)


def clear_edges(q):
    q[0:WIDTH, :] = jnp.zeros((WIDTH, 3 * CH), BF16)
    q[WIDTH + PIX : 2 * WIDTH + PIX, :] = jnp.zeros((WIDTH, 3 * CH), BF16)


def put_shifted(q, value):
    column = lax.broadcasted_iota(jnp.int32, (PIX, 1), 0) & (WIDTH - 1)
    before = jnp.where(column == 0, 0.0, pltpu.roll(value, 1, 0))
    after = jnp.where(column == WIDTH - 1, 0.0, pltpu.roll(value, PIX - 1, 0))
    q[WIDTH : WIDTH + PIX, 0:CH] = before.astype(BF16)
    q[WIDTH : WIDTH + PIX, CH : 2 * CH] = value.astype(BF16)
    q[WIDTH : WIDTH + PIX, 2 * CH : 3 * CH] = after.astype(BF16)


def conv(q, w):
    total = None
    for r in range(3):
        part = jnp.dot(q[WIDTH * r : WIDTH * r + PIX, :], w[3 * CH * r : 3 * CH * (r + 1), :], preferred_element_type=F32)
        total = part if total is None else total + part
    return total


def fwd_kernel(tick, aliased, *refs):
    names = ["sec", "x", "w1", "w2", "bias", "ones"]
    if tick >= 5:
        names.append("skip")
    if tick == 7:
        names.append("target")
    if aliased:
        names += ["_za", "_zb", "_sc"]
    names += ["y", "za", "zb", "sc"]
    names += ["xv", "w1v", "w2v", "biasv", "onesv", "skipv", "targetv", "q", "zav", "zbv", "scv", "yv", "sem"]
    r = dict(zip(names, refs, strict=True))

    @pl.when(r["sec"][0] == tick)
    def _():
        copies = {}
        loads = ["x", "ones", "w1", "bias", "w2"]
        if tick >= 5:
            loads.insert(1, "skip")
        if tick == 7:
            loads.append("target")
        for i, name in enumerate(loads):
            copies[name] = pltpu.make_async_copy(r[name], r[name + "v"], r["sem"].at[i])
            copies[name].start()
        clear_edges(r["q"])
        copies["x"].wait()
        x = unpack(r["xv"])
        if tick == 4:
            x = x + x
        if tick >= 5:
            copies["skip"].wait()
            x = x + unpack(r["skipv"])
        copies["ones"].wait()
        ones = r["onesv"][...]
        za, ra = normed(x, ones)
        r["zav"][...] = za
        save_a = pltpu.make_async_copy(r["zav"], r["za"], r["sem"].at[8])
        save_a.start()
        put_shifted(r["q"], za * sigmoid(za))
        copies["w1"].wait()
        copies["bias"].wait()
        mid = conv(r["q"], r["w1v"]) + r["biasv"][0:1, :]
        zb, rb = normed(mid, ones)
        r["zbv"][...] = zb
        save_b = pltpu.make_async_copy(r["zbv"], r["zb"], r["sem"].at[9])
        save_b.start()
        r["scv"][...] = jnp.concatenate([ra, rb, jnp.zeros((6, CH), F32)], axis=0)
        save_c = pltpu.make_async_copy(r["scv"], r["sc"], r["sem"].at[10])
        save_c.start()
        put_shifted(r["q"], zb * sigmoid(zb))
        copies["w2"].wait()
        y = x + conv(r["q"], r["w2v"])
        if tick == 7:
            copies["target"].wait()
            y = (y - r["targetv"][...].astype(F32)) * (1.0 / math.sqrt(PIX))
        pack(r["yv"], y)
        out = pltpu.make_async_copy(r["yv"], r["y"], r["sem"].at[11])
        out.start()
        save_a.wait()
        save_b.wait()
        save_c.wait()
        out.wait()


def forward(tick, sec, x, w1, w2, bias, ones, skip, target, saved):
    args = [sec, x, w1, w2, bias, ones]
    if tick >= 5:
        args.append(skip)
    if tick == 7:
        args.append(target)
    aliases = {}
    if saved is not None:
        aliases = {len(args) + i: 1 + i for i in range(3)}
        args += list(saved)
    image = jax.ShapeDtypeStruct((PIX, CH), F32)
    outs = pl.pallas_call(
        functools.partial(fwd_kernel, tick, saved is not None),
        out_shape=(jax.ShapeDtypeStruct((PACK, 128), F32), image, image, jax.ShapeDtypeStruct((8, CH), F32)),
        in_specs=[SMEM] + [ANY] * (len(args) - 1),
        out_specs=(ANY,) * 4,
        scratch_shapes=[
            pltpu.VMEM((PACK, 128), F32),
            pltpu.VMEM((KROWS, CH), BF16),
            pltpu.VMEM((KROWS, CH), BF16),
            pltpu.VMEM((8, CH), F32),
            pltpu.VMEM((CH, CH), BF16),
            pltpu.VMEM((PACK, 128), F32),
            pltpu.VMEM((PIX, CH), BF16),
            pltpu.VMEM((PIX + 2 * WIDTH, 3 * CH), BF16),
            pltpu.VMEM((PIX, CH), F32),
            pltpu.VMEM((PIX, CH), F32),
            pltpu.VMEM((8, CH), F32),
            pltpu.VMEM((PACK, 128), F32),
            pltpu.SemaphoreType.DMA((12,)),
        ],
        input_output_aliases=aliases,
        compiler_params=pltpu.CompilerParams(vmem_limit_bytes=24 << 20),
        cost_estimate=pl.CostEstimate(flops=4 * PIX * KROWS * CH, bytes_accessed=5 << 20, transcendentals=2 * PIX * CH),
        name="section_fwd",
    )(*args)
    return outs[0], outs[1:]


def bwd_kernel(tick, aliased, *refs):
    names = ["sec", "g", "w1t", "w2t", "ones", "za", "zb", "sc"]
    if tick < 3:
        names.append("skip")
    if aliased:
        names += ["_gb", "_gm", "_db"]
    if tick > 0:
        names.append("gu")
    names += ["gb", "gm", "db"]
    names += ["gv", "skipv", "w1tv", "w2tv", "onesv", "zav", "zbv", "scv", "q", "gbv", "gmv", "dbv", "guv", "sem"]
    r = dict(zip(names, refs, strict=True))

    @pl.when(r["sec"][0] == tick)
    def _():
        copies = {}
        loads = ["g", "w2t", "zb", "sc", "ones"]
        if tick < 3:
            loads.insert(1, "skip")
        if tick > 0:
            loads += ["w1t", "za"]
        for i, name in enumerate(loads):
            copies[name] = pltpu.make_async_copy(r[name], r[name + "v"], r["sem"].at[i])
            copies[name].start()
        clear_edges(r["q"])
        copies["g"].wait()
        g = unpack(r["gv"])
        if tick == 3:
            g = g + g
        if tick < 3:
            copies["skip"].wait()
            g = g + unpack(r["skipv"])
        r["gbv"][...] = g.astype(BF16)
        save_g = pltpu.make_async_copy(r["gbv"], r["gb"], r["sem"].at[8])
        save_g.start()
        put_shifted(r["q"], g)
        copies["w2t"].wait()
        cot = conv(r["q"], r["w2tv"])
        copies["zb"].wait()
        copies["sc"].wait()
        copies["ones"].wait()
        ones = r["onesv"][...]
        gm = norm_back(r["zbv"][...], r["scv"][1:2, :], cot, ones)
        r["gmv"][...] = gm.astype(BF16)
        save_m = pltpu.make_async_copy(r["gmv"], r["gm"], r["sem"].at[9])
        save_m.start()
        r["dbv"][...] = jnp.concatenate([colsum(gm), jnp.zeros((7, CH), F32)], axis=0)
        save_b = pltpu.make_async_copy(r["dbv"], r["db"], r["sem"].at[10])
        save_b.start()
        if tick > 0:
            put_shifted(r["q"], gm)
            copies["w1t"].wait()
            cot = conv(r["q"], r["w1tv"])
            copies["za"].wait()
            gu = g + norm_back(r["zav"][...], r["scv"][0:1, :], cot, ones)
            pack(r["guv"], gu)
            out = pltpu.make_async_copy(r["guv"], r["gu"], r["sem"].at[11])
            out.start()
            out.wait()
        save_g.wait()
        save_m.wait()
        save_b.wait()


def backward(tick, sec, g, w1t, w2t, ones, kept, skip, saved):
    args = [sec, g, w1t, w2t, ones, *kept]
    if tick < 3:
        args.append(skip)
    first = 1 if tick > 0 else 0
    aliases = {}
    if saved is not None:
        aliases = {len(args) + i: first + i for i in range(3)}
        args += list(saved)
    low = jax.ShapeDtypeStruct((PIX, CH), BF16)
    out_shape = (low, low, jax.ShapeDtypeStruct((8, CH), F32))
    if tick > 0:
        out_shape = (jax.ShapeDtypeStruct((PACK, 128), F32),) + out_shape
    outs = pl.pallas_call(
        functools.partial(bwd_kernel, tick, saved is not None),
        out_shape=out_shape,
        in_specs=[SMEM] + [ANY] * (len(args) - 1),
        out_specs=(ANY,) * len(out_shape),
        scratch_shapes=[
            pltpu.VMEM((PACK, 128), F32),
            pltpu.VMEM((PACK, 128), F32),
            pltpu.VMEM((KROWS, CH), BF16),
            pltpu.VMEM((KROWS, CH), BF16),
            pltpu.VMEM((CH, CH), BF16),
            pltpu.VMEM((PIX, CH), F32),
            pltpu.VMEM((PIX, CH), F32),
            pltpu.VMEM((8, CH), F32),
            pltpu.VMEM((PIX + 2 * WIDTH, 3 * CH), BF16),
            pltpu.VMEM((PIX, CH), BF16),
            pltpu.VMEM((PIX, CH), BF16),
            pltpu.VMEM((8, CH), F32),
            pltpu.VMEM((PACK, 128), F32),
            pltpu.SemaphoreType.DMA((12,)),
        ],
        input_output_aliases=aliases,
        compiler_params=pltpu.CompilerParams(vmem_limit_bytes=24 << 20),
        cost_estimate=pl.CostEstimate(flops=4 * PIX * KROWS * CH, bytes_accessed=5 << 20, transcendentals=2 * PIX * CH),
        name="section_bwd",
    )(*args)
    return (outs[0] if tick > 0 else None), outs[first:]


def grad_kernel(z0, z1, g0, g1, out, q, at):
    r = pl.program_id(0)

    @pl.when(r == 0)
    def _():
        for i, (z, g) in enumerate(((z0, g0), (z1, g1))):
            clear_edges(q.at[i])
            put_shifted(q.at[i], g[...].astype(F32))
            value = z[...]
            at[i] = jnp.transpose(value * sigmoid(value)).astype(BF16)

    start = pl.multiple_of(WIDTH * (2 - r), WIDTH)
    total = jnp.dot(at[0], q[0, pl.ds(start, PIX), :], preferred_element_type=F32)
    total += jnp.dot(at[1], q[1, pl.ds(start, PIX), :], preferred_element_type=F32)
    for k in range(7):
        out[CH * k : CH * (k + 1), :] = total[:, 128 * k : 128 * (k + 1)]
    half = CH // 2
    out[7 * CH :, :] = jnp.concatenate([total[:half, 896:960], total[half:, 896:960]], axis=1)


def weight_grad(z0, z1, g0, g1):
    whole = pl.BlockSpec((PIX, CH), lambda r: (0, 0))
    return pl.pallas_call(
        grad_kernel,
        grid=(3,),
        out_shape=jax.ShapeDtypeStruct((GROWS, 128), F32),
        in_specs=[whole] * 4,
        out_specs=pl.BlockSpec((GROWS // 3, 128), lambda r: (r, 0)),
        scratch_shapes=[
            pltpu.VMEM((2, PIX + 2 * WIDTH, 3 * CH), BF16),
            pltpu.VMEM((2, CH, PIX), BF16),
        ],
        compiler_params=pltpu.CompilerParams(vmem_limit_bytes=24 << 20),
        cost_estimate=pl.CostEstimate(flops=4 * PIX * KROWS * CH, bytes_accessed=5 << 20, transcendentals=2 * PIX * CH),
        name="weight_grad",
    )(z0, z1, g0, g1)


def unpack_kernel(src, out):
    tail = src[7 * CH :, :]
    last = jnp.concatenate([tail[:, :64], tail[:, 64:]], axis=0)
    value = jnp.concatenate([src[CH * k : CH * (k + 1), :] for k in range(7)] + [last], axis=1)
    for c in range(3):
        out[0, CH * c : CH * (c + 1), :] = value[:, CH * (2 - c) : CH * (3 - c)]


def unpack_grad(packed, first):
    return pl.pallas_call(
        unpack_kernel,
        grid=(3,),
        out_shape=jax.ShapeDtypeStruct((1, KROWS, CH), F32),
        in_specs=[pl.BlockSpec((GROWS // 3, 128), lambda r: (3 * first + r, 0))],
        out_specs=pl.BlockSpec((1, KROWS // 3, CH), lambda r: (0, r, 0)),
        compiler_params=pltpu.CompilerParams(vmem_limit_bytes=24 << 20),
        name="unpack_grad",
    )(packed)


def embed_times(times):
    middle = TE // 2
    freqs = jnp.exp(-math.log(10000.0) * jnp.arange(middle, dtype=F32) / middle)
    angles = times.astype(F32)[:, None] * freqs[None, :]
    return jnp.concatenate([jnp.cos(angles), jnp.sin(angles)], axis=1)


def packed_image(image):
    half = PIX // 2
    tail = jnp.concatenate([image[:half, 256:320], image[half:, 256:320]], axis=1)
    return jnp.concatenate([image[:, 0:128], image[:, 128:256], tail], axis=0)


def turned(weight):
    taps = weight.reshape(9, CH, CH)[::-1]
    return jnp.transpose(taps, (0, 2, 1)).reshape(KROWS, CH)


def reduced(packed):
    part = lax.psum_scatter(packed, "core", scatter_dimension=0, tiled=True)
    part = lax.psum_scatter(part, "z", scatter_dimension=0, tiled=True)
    part = lax.psum(part, "x_hi")
    part = lax.all_gather(part, "z", axis=0, tiled=True)
    return lax.all_gather(part, "core", axis=0, tiled=True)


def local(features, target, timesteps, conv_one, conv_two, time_proj):
    sec = jnp.full((1,), lax.axis_index("section"), jnp.int32)
    w1, w2 = conv_one[0], conv_two[0]
    lanes = jnp.arange(CH) // (CH // GROUPS)
    ones = (lanes[:, None] == lanes[None, :]).astype(BF16)
    embedded = embed_times(timesteps)
    bias = jnp.dot(embedded, time_proj[0], precision=lax.Precision.HIGHEST)
    bias = jnp.broadcast_to(bias[:, None, :], (MICRO, 8, CH))
    images = features.reshape(MICRO, PIX, CH).astype(F32)
    targets = target.reshape(MICRO, PIX, CH)

    arrived = [packed_image(images[m]) for m in range(MICRO)]
    kept = [None] * MICRO
    skips = {}
    for tick in range(8):
        sent = [None] * MICRO
        for m in range(MICRO):
            skip = skips[7 - tick, m] if tick >= 5 else None
            sent[m], kept[m] = forward(tick, sec, arrived[m], w1, w2, bias[m], ones, skip, targets[m], kept[m])
            if tick < 7:
                arrived[m] = lax.ppermute(sent[m], "section", [(tick, tick + 1)])
        if tick < 3:
            tied = lax.optimization_barrier((tuple(sent), tuple(arrived)))[0]
            for m in range(MICRO):
                skips[tick, m] = lax.ppermute(tied[m], "section", [(tick, 7 - tick)])

    w1t, w2t, _ = lax.optimization_barrier((w1, w2, arrived[0]))
    w1t, w2t = turned(w1t), turned(w2t)
    arrived = sent
    saved = [None] * MICRO
    skips = {}
    for tick in range(7, -1, -1):
        sent = [None] * MICRO
        for m in range(MICRO):
            skip = skips[tick, m] if tick < 3 else None
            sent[m], saved[m] = backward(tick, sec, arrived[m], w1t, w2t, ones, kept[m], skip, saved[m])
            if tick > 0:
                arrived[m] = lax.ppermute(sent[m], "section", [(tick, tick - 1)])
        if tick > 4:
            tied = lax.optimization_barrier((tuple(sent), tuple(arrived)))[0]
            for m in range(MICRO):
                skips[7 - tick, m] = lax.ppermute(tied[m], "section", [(tick, 7 - tick)])

    grad_two = weight_grad(kept[0][1], kept[1][1], saved[0][0], saved[1][0])
    grad_one = weight_grad(kept[0][0], kept[1][0], saved[0][1], saved[1][1])
    grad_bias = jnp.concatenate([saved[m][2][0:1] for m in range(MICRO)], axis=0)
    grad_time = jnp.dot(embedded.T, grad_bias, precision=lax.Precision.HIGHEST)
    rest = jnp.zeros((TOTAL - 2 * GROWS - TROWS, 128), F32)
    total = reduced(jnp.concatenate([grad_one, grad_two, grad_time.reshape(TROWS, 128), rest], axis=0))
    sum_time = total[2 * GROWS : 2 * GROWS + TROWS].reshape(1, TE, CH)
    return unpack_grad(total, 0), unpack_grad(total, 1), sum_time


def solution(mesh):
    inner = Mesh(mesh.devices.reshape(2, 8, 2, 8), ("x_hi", "z", "core", "section"))
    batch = ("x_hi", "z", "core")
    by_section = P("section", None, None)
    return jax.shard_map(
        local,
        mesh=inner,
        in_specs=(P(batch, None, None), P(batch, None, None), P(batch), by_section, by_section, by_section),
        out_specs=(by_section, by_section, by_section),
        check_vma=False,
    )
```

```python
import functools
import math

import jax
import jax.numpy as jnp
from jax import lax
from jax.experimental import pallas as pl
from jax.experimental.pallas import tpu as pltpu
from jax.sharding import Mesh
from jax.sharding import PartitionSpec as P

CH = 320
TE = 320
GROUPS = 32
HEIGHT = 16
WIDTH = 16
PIX = HEIGHT * WIDTH
KROWS = 9 * CH
MICRO = 2
PACK = PIX * CH // 128
GROWS = KROWS * CH // 128
HALF = 3840
F32 = jnp.float32
BF16 = jnp.bfloat16
ANY = pl.BlockSpec(memory_space=pl.ANY)
SMEM = pl.BlockSpec(memory_space=pltpu.SMEM)


def unpack(ref):
    tail = ref[2 * PIX : PACK, :]
    last = jnp.concatenate([tail[:, :64], tail[:, 64:]], axis=0)
    return jnp.concatenate([ref[0:PIX, :], ref[PIX : 2 * PIX, :], last], axis=1)


def pack(ref, value):
    ref[0:PIX, :] = value[:, 0:128]
    ref[PIX : 2 * PIX, :] = value[:, 128:256]
    half = PIX // 2
    ref[2 * PIX : PACK, :] = jnp.concatenate([value[:half, 256:320], value[half:, 256:320]], axis=1)


def split3(row):
    high = row.astype(BF16).astype(F32)
    rest = row - high
    mid = rest.astype(BF16).astype(F32)
    return [high, mid, rest - mid]


def group_mean(rows, ones):
    parts = []
    for row in rows:
        parts += split3(row)
    parts += [jnp.zeros_like(rows[0])] * (8 - len(parts))
    sums = jnp.dot(jnp.concatenate(parts, axis=0).astype(BF16), ones, preferred_element_type=F32)
    scale = 1.0 / (PIX * (CH // GROUPS))
    return [(sums[3 * i : 3 * i + 1] + sums[3 * i + 1 : 3 * i + 2] + sums[3 * i + 2 : 3 * i + 3]) * scale for i in range(len(rows))]


def colsum(value):
    return jnp.sum(value, axis=0, keepdims=True)


def normed(value, ones):
    (center,) = group_mean([colsum(value)], ones)
    value = value - center
    (spread,) = group_mean([colsum(value * value)], ones)
    scale = lax.rsqrt(spread + 1e-05)
    return value * scale, scale


def sigmoid(z):
    return 1.0 / (1.0 + jnp.exp(-z))


def norm_back(z, scale, cot, ones):
    gate = sigmoid(z)
    cot = cot * (gate * (1.0 + z * (1.0 - gate)))
    mean_one, mean_two = group_mean([colsum(cot), colsum(cot * z)], ones)
    return scale * (cot - mean_one - z * mean_two)


def clear_edges(q):
    q[0:WIDTH, :] = jnp.zeros((WIDTH, 3 * CH), BF16)
    q[WIDTH + PIX : 2 * WIDTH + PIX, :] = jnp.zeros((WIDTH, 3 * CH), BF16)


def put_shifted(q, value):
    column = lax.broadcasted_iota(jnp.int32, (PIX, 1), 0) & (WIDTH - 1)
    before = jnp.where(column == 0, 0.0, pltpu.roll(value, 1, 0))
    after = jnp.where(column == WIDTH - 1, 0.0, pltpu.roll(value, PIX - 1, 0))
    q[WIDTH : WIDTH + PIX, 0:CH] = before.astype(BF16)
    q[WIDTH : WIDTH + PIX, CH : 2 * CH] = value.astype(BF16)
    q[WIDTH : WIDTH + PIX, 2 * CH : 3 * CH] = after.astype(BF16)


def conv(q, w, acc):
    acc[...] = jnp.zeros((PIX, CH), F32)

    def body(r, carry):
        rows = pl.multiple_of(WIDTH * r, WIDTH)
        taps = pl.multiple_of(3 * CH * r, 3 * CH)
        acc[...] += jnp.dot(q[pl.ds(rows, PIX), :], w[pl.ds(taps, 3 * CH), :], preferred_element_type=F32)
        return carry

    lax.fori_loop(0, 3, body, 0)
    return acc[...]


def fwd_kernel(tick, aliased, *refs):
    names = ["sec", "x", "w1", "w2", "bias", "ones"]
    if tick >= 5:
        names.append("skip")
    if tick == 7:
        names.append("target")
    if aliased:
        names += ["_za", "_zb", "_sc"]
    names += ["y", "za", "zb", "sc"]
    names += ["xv", "w1v", "w2v", "biasv", "onesv", "skipv", "targetv", "q", "zav", "zbv", "scv", "yv", "acc", "sem"]
    r = dict(zip(names, refs, strict=True))

    @pl.when(r["sec"][0] == tick)
    def _():
        copies = {}
        loads = ["x", "ones", "w1", "bias", "w2"]
        if tick >= 5:
            loads.insert(1, "skip")
        if tick == 7:
            loads.append("target")
        for i, name in enumerate(loads):
            copies[name] = pltpu.make_async_copy(r[name], r[name + "v"], r["sem"].at[i])
            copies[name].start()
        clear_edges(r["q"])
        copies["x"].wait()
        x = unpack(r["xv"])
        if tick == 4:
            x = x + x
        if tick >= 5:
            copies["skip"].wait()
            x = x + unpack(r["skipv"])
        copies["ones"].wait()
        ones = r["onesv"][...]
        za, ra = normed(x, ones)
        r["zav"][...] = za
        save_a = pltpu.make_async_copy(r["zav"], r["za"], r["sem"].at[8])
        save_a.start()
        put_shifted(r["q"], za * sigmoid(za))
        copies["w1"].wait()
        copies["bias"].wait()
        mid = conv(r["q"], r["w1v"], r["acc"]) + r["biasv"][0:1, :]
        zb, rb = normed(mid, ones)
        r["zbv"][...] = zb
        save_b = pltpu.make_async_copy(r["zbv"], r["zb"], r["sem"].at[9])
        save_b.start()
        r["scv"][...] = jnp.concatenate([ra, rb, jnp.zeros((6, CH), F32)], axis=0)
        save_c = pltpu.make_async_copy(r["scv"], r["sc"], r["sem"].at[10])
        save_c.start()
        put_shifted(r["q"], zb * sigmoid(zb))
        copies["w2"].wait()
        y = x + conv(r["q"], r["w2v"], r["acc"])
        if tick == 7:
            copies["target"].wait()
            y = (y - r["targetv"][...].astype(F32)) * (1.0 / math.sqrt(PIX))
        pack(r["yv"], y)
        out = pltpu.make_async_copy(r["yv"], r["y"], r["sem"].at[11])
        out.start()
        save_a.wait()
        save_b.wait()
        save_c.wait()
        out.wait()


def forward(tick, sec, x, w1, w2, bias, ones, skip, target, saved):
    args = [sec, x, w1, w2, bias, ones]
    if tick >= 5:
        args.append(skip)
    if tick == 7:
        args.append(target)
    aliases = {}
    if saved is not None:
        aliases = {len(args) + i: 1 + i for i in range(3)}
        args += list(saved)
    image = jax.ShapeDtypeStruct((PIX, CH), F32)
    outs = pl.pallas_call(
        functools.partial(fwd_kernel, tick, saved is not None),
        out_shape=(jax.ShapeDtypeStruct((PACK, 128), F32), image, image, jax.ShapeDtypeStruct((8, CH), F32)),
        in_specs=[SMEM] + [ANY] * (len(args) - 1),
        out_specs=(ANY,) * 4,
        scratch_shapes=[
            pltpu.VMEM((PACK, 128), F32),
            pltpu.VMEM((KROWS, CH), BF16),
            pltpu.VMEM((KROWS, CH), BF16),
            pltpu.VMEM((8, CH), F32),
            pltpu.VMEM((CH, CH), BF16),
            pltpu.VMEM((PACK, 128), F32),
            pltpu.VMEM((PIX, CH), BF16),
            pltpu.VMEM((PIX + 2 * WIDTH, 3 * CH), BF16),
            pltpu.VMEM((PIX, CH), F32),
            pltpu.VMEM((PIX, CH), F32),
            pltpu.VMEM((8, CH), F32),
            pltpu.VMEM((PACK, 128), F32),
            pltpu.VMEM((PIX, CH), F32),
            pltpu.SemaphoreType.DMA((12,)),
        ],
        input_output_aliases=aliases,
        compiler_params=pltpu.CompilerParams(vmem_limit_bytes=24 << 20),
        cost_estimate=pl.CostEstimate(flops=4 * PIX * KROWS * CH, bytes_accessed=5 << 20, transcendentals=2 * PIX * CH),
        name="section_fwd",
    )(*args)
    return outs[0], outs[1:]


def bwd_kernel(tick, aliased, *refs):
    names = ["sec", "g", "w1t", "w2t", "ones", "za", "zb", "sc"]
    if tick < 3:
        names.append("skip")
    if aliased:
        names += ["_gb", "_gm", "_db"]
    if tick > 0:
        names.append("gu")
    names += ["gb", "gm", "db"]
    names += ["gv", "skipv", "w1tv", "w2tv", "onesv", "zav", "zbv", "scv", "q", "gbv", "gmv", "dbv", "guv", "acc", "sem"]
    r = dict(zip(names, refs, strict=True))

    @pl.when(r["sec"][0] == tick)
    def _():
        copies = {}
        loads = ["g", "w2t", "zb", "sc", "ones"]
        if tick < 3:
            loads.insert(1, "skip")
        if tick > 0:
            loads += ["w1t", "za"]
        for i, name in enumerate(loads):
            copies[name] = pltpu.make_async_copy(r[name], r[name + "v"], r["sem"].at[i])
            copies[name].start()
        clear_edges(r["q"])
        copies["g"].wait()
        g = unpack(r["gv"])
        if tick == 3:
            g = g + g
        if tick < 3:
            copies["skip"].wait()
            g = g + unpack(r["skipv"])
        r["gbv"][...] = g.astype(BF16)
        save_g = pltpu.make_async_copy(r["gbv"], r["gb"], r["sem"].at[8])
        save_g.start()
        put_shifted(r["q"], g)
        copies["w2t"].wait()
        cot = conv(r["q"], r["w2tv"], r["acc"])
        copies["zb"].wait()
        copies["sc"].wait()
        copies["ones"].wait()
        ones = r["onesv"][...]
        gm = norm_back(r["zbv"][...], r["scv"][1:2, :], cot, ones)
        r["gmv"][...] = gm.astype(BF16)
        save_m = pltpu.make_async_copy(r["gmv"], r["gm"], r["sem"].at[9])
        save_m.start()
        r["dbv"][...] = jnp.concatenate([colsum(gm), jnp.zeros((7, CH), F32)], axis=0)
        save_b = pltpu.make_async_copy(r["dbv"], r["db"], r["sem"].at[10])
        save_b.start()
        if tick > 0:
            put_shifted(r["q"], gm)
            copies["w1t"].wait()
            cot = conv(r["q"], r["w1tv"], r["acc"])
            copies["za"].wait()
            gu = g + norm_back(r["zav"][...], r["scv"][0:1, :], cot, ones)
            pack(r["guv"], gu)
            out = pltpu.make_async_copy(r["guv"], r["gu"], r["sem"].at[11])
            out.start()
            out.wait()
        save_g.wait()
        save_m.wait()
        save_b.wait()


def backward(tick, sec, g, w1t, w2t, ones, kept, skip, saved):
    args = [sec, g, w1t, w2t, ones, *kept]
    if tick < 3:
        args.append(skip)
    first = 1 if tick > 0 else 0
    aliases = {}
    if saved is not None:
        aliases = {len(args) + i: first + i for i in range(3)}
        args += list(saved)
    low = jax.ShapeDtypeStruct((PIX, CH), BF16)
    out_shape = (low, low, jax.ShapeDtypeStruct((8, CH), F32))
    if tick > 0:
        out_shape = (jax.ShapeDtypeStruct((PACK, 128), F32),) + out_shape
    outs = pl.pallas_call(
        functools.partial(bwd_kernel, tick, saved is not None),
        out_shape=out_shape,
        in_specs=[SMEM] + [ANY] * (len(args) - 1),
        out_specs=(ANY,) * len(out_shape),
        scratch_shapes=[
            pltpu.VMEM((PACK, 128), F32),
            pltpu.VMEM((PACK, 128), F32),
            pltpu.VMEM((KROWS, CH), BF16),
            pltpu.VMEM((KROWS, CH), BF16),
            pltpu.VMEM((CH, CH), BF16),
            pltpu.VMEM((PIX, CH), F32),
            pltpu.VMEM((PIX, CH), F32),
            pltpu.VMEM((8, CH), F32),
            pltpu.VMEM((PIX + 2 * WIDTH, 3 * CH), BF16),
            pltpu.VMEM((PIX, CH), BF16),
            pltpu.VMEM((PIX, CH), BF16),
            pltpu.VMEM((8, CH), F32),
            pltpu.VMEM((PACK, 128), F32),
            pltpu.VMEM((PIX, CH), F32),
            pltpu.SemaphoreType.DMA((12,)),
        ],
        input_output_aliases=aliases,
        compiler_params=pltpu.CompilerParams(vmem_limit_bytes=24 << 20),
        cost_estimate=pl.CostEstimate(flops=4 * PIX * KROWS * CH, bytes_accessed=5 << 20, transcendentals=2 * PIX * CH),
        name="section_bwd",
    )(*args)
    return (outs[0] if tick > 0 else None), outs[first:]


def grad_kernel(z0, z1, g0, g1, out, q, gt, whole):
    for i, (z, g) in enumerate(((z0, g0), (z1, g1))):
        clear_edges(q.at[i])
        value = z[...]
        put_shifted(q.at[i], value * sigmoid(value))
        gt[i] = jnp.transpose(g[...].astype(F32)).astype(BF16)
    for r in range(3):
        part = jnp.dot(gt[0], q[0, WIDTH * r : WIDTH * r + PIX, :], preferred_element_type=F32)
        part += jnp.dot(gt[1], q[1, WIDTH * r : WIDTH * r + PIX, :], preferred_element_type=F32)
        whole[:, 3 * CH * r : 3 * CH * (r + 1)] = part
    for k in range(22):
        out[CH * k : CH * (k + 1), :] = whole[:, 128 * k : 128 * (k + 1)]
    half = CH // 2
    out[22 * CH : GROWS, :] = jnp.concatenate([whole[:half, 2816:2880], whole[half:, 2816:2880]], axis=1)


def weight_grad(z0, z1, g0, g1):
    return pl.pallas_call(
        grad_kernel,
        out_shape=jax.ShapeDtypeStruct((2 * HALF, 128), F32),
        scratch_shapes=[
            pltpu.VMEM((2, PIX + 2 * WIDTH, 3 * CH), BF16),
            pltpu.VMEM((2, CH, PIX), BF16),
            pltpu.VMEM((CH, KROWS), F32),
        ],
        compiler_params=pltpu.CompilerParams(vmem_limit_bytes=24 << 20),
        cost_estimate=pl.CostEstimate(flops=4 * PIX * KROWS * CH, bytes_accessed=5 << 20, transcendentals=2 * PIX * CH),
        name="weight_grad",
    )(z0, z1, g0, g1)


def unpack_kernel(core, mine, other, out):
    def write(low, high):
        for k in range(12):
            out[0, :, 128 * k : 128 * (k + 1)] = low[CH * k : CH * (k + 1), :]
        for k in range(10):
            out[0, :, 1536 + 128 * k : 1536 + 128 * (k + 1)] = high[CH * k : CH * (k + 1), :]
        tail = high[10 * CH : 10 * CH + CH // 2, :]
        out[0, :, 2816:2880] = jnp.concatenate([tail[:, :64], tail[:, 64:]], axis=0)

    @pl.when(core[0] == 0)
    def _():
        write(mine, other)

    @pl.when(core[0] == 1)
    def _():
        write(other, mine)


def unpack_grad(core, mine, other):
    vmem = pl.BlockSpec(memory_space=pltpu.VMEM)
    turned_out = pl.pallas_call(
        unpack_kernel,
        out_shape=jax.ShapeDtypeStruct((1, CH, KROWS), F32),
        in_specs=[SMEM, vmem, vmem],
        out_specs=vmem,
        compiler_params=pltpu.CompilerParams(vmem_limit_bytes=24 << 20),
        name="unpack_grad",
    )(core, mine, other)
    return jnp.swapaxes(turned_out, 1, 2)


def embed_times(times):
    middle = TE // 2
    freqs = jnp.exp(-math.log(10000.0) * jnp.arange(middle, dtype=F32) / middle)
    angles = times.astype(F32)[:, None] * freqs[None, :]
    return jnp.concatenate([jnp.cos(angles), jnp.sin(angles)], axis=1)


def packed_image(image):
    half = PIX // 2
    tail = jnp.concatenate([image[:half, 256:320], image[half:, 256:320]], axis=1)
    return jnp.concatenate([image[:, 0:128], image[:, 128:256], tail], axis=0)


def turned(weight):
    taps = weight.reshape(9, CH, CH)[::-1]
    return jnp.transpose(taps, (0, 2, 1)).reshape(KROWS, CH)


def along_z(value, sign):
    pairs = []
    for z in range(8):
        pairs += [(2 * z, 2 * ((z + sign) % 8)), (2 * z + 1, 2 * ((z - sign) % 8) + 1)]
    return lax.ppermute(value, ("z", "core"), pairs)


def reduced(streams):
    core, z = lax.axis_index("core"), lax.axis_index("z")
    way = 1 - 2 * core
    swap = [(0, 1), (1, 0)]

    def chunk(blocks, ahead):
        return lax.dynamic_index_in_dim(blocks, (z + way * ahead + 8) % 8, 0, keepdims=False)

    mine = []
    for packed in streams:
        halves = packed.reshape(2, HALF, 128)
        given = lax.dynamic_index_in_dim(halves, 1 - core, 0, keepdims=False)
        kept = lax.dynamic_index_in_dim(halves, core, 0, keepdims=False)
        mine.append((kept + lax.ppermute(given, "core", swap)).reshape(8, HALF // 8, 128))
    forth = [chunk(blocks, 4) for blocks in mine]
    back = [chunk(blocks, -3) for blocks in mine]
    for step in range(1, 5):
        for i, blocks in enumerate(mine):
            forth[i] = along_z(forth[i], 1)
            if step < 4:
                forth[i] = forth[i] + chunk(blocks, 4 - step)
                back[i] = along_z(back[i], -1)
            if step < 3:
                back[i] = back[i] + chunk(blocks, step - 3)
    total = []
    for i, blocks in enumerate(mine):
        part = forth[i] + back[i] + chunk(blocks, 0)
        total.append(part + lax.ppermute(part, "x_hi", swap))
    whole = [lax.dynamic_update_index_in_dim(jnp.zeros_like(blocks), part, z, 0) for blocks, part in zip(mine, total)]
    forth, back = list(total), list(total)
    for step in range(1, 5):
        for i in range(len(total)):
            forth[i] = along_z(forth[i], 1)
            whole[i] = lax.dynamic_update_index_in_dim(whole[i], forth[i], (z - way * step + 8) % 8, 0)
            if step < 4:
                back[i] = along_z(back[i], -1)
                whole[i] = lax.dynamic_update_index_in_dim(whole[i], back[i], (z + way * step + 8) % 8, 0)
    result = []
    for blocks in whole:
        flat = blocks.reshape(HALF, 128)
        result.append((flat, lax.ppermute(flat, "core", swap)))
    return result


def crossed(sec, sent_by, arrived, pairs):
    sent_by = lax.optimization_barrier((sent_by, tuple(arrived)))[0]
    ticks = sorted(sent_by)
    moved = []
    for m in range(MICRO):
        value = sent_by[ticks[0]][m]
        for tick in ticks[1:]:
            value = jnp.where(sec[0] == tick, sent_by[tick][m], value)
        moved.append(lax.ppermute(value, "section", pairs))
    return moved


def local(features, target, timesteps, conv_one, conv_two, time_proj):
    sec = jnp.full((1,), lax.axis_index("section"), jnp.int32)
    w1, w2 = conv_one[0], conv_two[0]
    lanes = jnp.arange(CH) // (CH // GROUPS)
    ones = (lanes[:, None] == lanes[None, :]).astype(BF16)
    embedded = embed_times(timesteps)
    bias = jnp.dot(embedded, time_proj[0], precision=lax.Precision.HIGHEST)
    bias = jnp.broadcast_to(bias[:, None, :], (MICRO, 8, CH))
    images = features.reshape(MICRO, PIX, CH).astype(F32)
    targets = target.reshape(MICRO, PIX, CH)

    arrived = [packed_image(images[m]) for m in range(MICRO)]
    kept = [None] * MICRO
    sent_by = {}
    skips = None
    for tick in range(8):
        sent = [None] * MICRO
        for m in range(MICRO):
            skip = skips[m] if tick >= 5 else None
            sent[m], kept[m] = forward(tick, sec, arrived[m], w1, w2, bias[m], ones, skip, targets[m], kept[m])
            if tick < 7:
                arrived[m] = lax.ppermute(sent[m], "section", [(tick, tick + 1)])
        if tick == 0:
            w1t, w2t, _ = lax.optimization_barrier((w1, w2, sent[0]))
            w1t, w2t = turned(w1t), turned(w2t)
        if tick < 3:
            sent_by[tick] = tuple(sent)
        if tick == 2:
            skips = crossed(sec, sent_by, arrived, [(0, 7), (1, 6), (2, 5)])

    arrived = sent
    saved = [None] * MICRO
    sent_by = {}
    for tick in range(7, -1, -1):
        sent = [None] * MICRO
        for m in range(MICRO):
            skip = skips[m] if tick < 3 else None
            sent[m], saved[m] = backward(tick, sec, arrived[m], w1t, w2t, ones, kept[m], skip, saved[m])
            if tick > 0:
                arrived[m] = lax.ppermute(sent[m], "section", [(tick, tick - 1)])
        if tick > 4:
            sent_by[tick] = tuple(sent)
        if tick == 5:
            skips = crossed(sec, sent_by, arrived, [(7, 0), (6, 1), (5, 2)])

    grad_two = weight_grad(kept[0][1], kept[1][1], saved[0][0], saved[1][0])
    grad_one = weight_grad(kept[0][0], kept[1][0], saved[0][1], saved[1][1])
    grad_bias = jnp.concatenate([saved[m][2][0:1] for m in range(MICRO)], axis=0)
    grad_time = jnp.dot(embedded.T, grad_bias, precision=lax.Precision.HIGHEST)
    sum_time = lax.psum(grad_time, ("x_hi", "z", "core"))
    (two, one) = reduced([grad_two, grad_one])
    core = jnp.full((1,), lax.axis_index("core"), jnp.int32)
    return unpack_grad(core, *one), unpack_grad(core, *two), sum_time[None]


def solution(mesh):
    inner = Mesh(mesh.devices.reshape(2, 8, 2, 8), ("x_hi", "z", "core", "section"))
    batch = ("x_hi", "z", "core")
    by_section = P("section", None, None)
    return jax.shard_map(
        local,
        mesh=inner,
        in_specs=(P(batch, None, None), P(batch, None, None), P(batch), by_section, by_section, by_section),
        out_specs=(by_section, by_section, by_section),
        check_vma=False,
    )
```

```python
import functools
import math

import jax
import jax.numpy as jnp
from jax import lax
from jax.experimental import pallas as pl
from jax.experimental.pallas import tpu as pltpu
from jax.sharding import Mesh
from jax.sharding import PartitionSpec as P

CH = 320
TE = 320
GROUPS = 32
HEIGHT = 16
WIDTH = 16
PIX = HEIGHT * WIDTH
KROWS = 9 * CH
MICRO = 2
PACK = PIX * CH // 128
GROWS = KROWS * CH // 128
HALF = 3840
F32 = jnp.float32
BF16 = jnp.bfloat16
ANY = pl.BlockSpec(memory_space=pl.ANY)
SMEM = pl.BlockSpec(memory_space=pltpu.SMEM)


def unpack(ref):
    tail = ref[2 * PIX : PACK, :]
    last = jnp.concatenate([tail[:, :64], tail[:, 64:]], axis=0)
    return jnp.concatenate([ref[0:PIX, :], ref[PIX : 2 * PIX, :], last], axis=1)


def pack(ref, value):
    ref[0:PIX, :] = value[:, 0:128]
    ref[PIX : 2 * PIX, :] = value[:, 128:256]
    half = PIX // 2
    ref[2 * PIX : PACK, :] = jnp.concatenate([value[:half, 256:320], value[half:, 256:320]], axis=1)


def split3(row):
    high = row.astype(BF16).astype(F32)
    rest = row - high
    mid = rest.astype(BF16).astype(F32)
    return [high, mid, rest - mid]


def group_mean(rows, ones):
    parts = []
    for row in rows:
        parts += split3(row)
    parts += [jnp.zeros_like(rows[0])] * (8 - len(parts))
    sums = jnp.dot(jnp.concatenate(parts, axis=0).astype(BF16), ones, preferred_element_type=F32)
    scale = 1.0 / (PIX * (CH // GROUPS))
    return [(sums[3 * i : 3 * i + 1] + sums[3 * i + 1 : 3 * i + 2] + sums[3 * i + 2 : 3 * i + 3]) * scale for i in range(len(rows))]


def colsum(value):
    return jnp.sum(value, axis=0, keepdims=True)


def normed(value, ones):
    (center,) = group_mean([colsum(value)], ones)
    value = value - center
    (spread,) = group_mean([colsum(value * value)], ones)
    scale = lax.rsqrt(spread + 1e-05)
    return value * scale, scale


def sigmoid(z):
    return 1.0 / (1.0 + jnp.exp(-z))


def norm_back(z, scale, cot, ones):
    gate = sigmoid(z)
    cot = cot * (gate * (1.0 + z * (1.0 - gate)))
    mean_one, mean_two = group_mean([colsum(cot), colsum(cot * z)], ones)
    return scale * (cot - mean_one - z * mean_two)


def clear_edges(q):
    q[0:WIDTH, :] = jnp.zeros((WIDTH, 3 * CH), BF16)
    q[WIDTH + PIX : 2 * WIDTH + PIX, :] = jnp.zeros((WIDTH, 3 * CH), BF16)


def put_shifted(q, value):
    column = lax.broadcasted_iota(jnp.int32, (PIX, 1), 0) & (WIDTH - 1)
    before = jnp.where(column == 0, 0.0, pltpu.roll(value, 1, 0))
    after = jnp.where(column == WIDTH - 1, 0.0, pltpu.roll(value, PIX - 1, 0))
    q[WIDTH : WIDTH + PIX, 0:CH] = before.astype(BF16)
    q[WIDTH : WIDTH + PIX, CH : 2 * CH] = value.astype(BF16)
    q[WIDTH : WIDTH + PIX, 2 * CH : 3 * CH] = after.astype(BF16)


def conv(q, w):
    total = None
    for r in range(3):
        part = jnp.dot(q[WIDTH * r : WIDTH * r + PIX, :], w[3 * CH * r : 3 * CH * (r + 1), :], preferred_element_type=F32)
        total = part if total is None else total + part
    return total


def fwd_kernel(tick, aliased, *refs):
    names = ["sec", "x", "w1", "w2", "bias", "ones"]
    if tick >= 5:
        names.append("skip")
    if tick == 7:
        names.append("target")
    if aliased:
        names += ["_za", "_zb", "_sc"]
    names += ["y", "za", "zb", "sc"]
    names += ["xv", "w1v", "w2v", "biasv", "onesv", "skipv", "targetv", "q", "zav", "zbv", "scv", "yv", "sem"]
    r = dict(zip(names, refs, strict=True))

    @pl.when(r["sec"][0] == tick)
    def _():
        copies = {}
        loads = ["x", "ones", "w1", "bias", "w2"]
        if tick >= 5:
            loads.insert(1, "skip")
        if tick == 7:
            loads.append("target")
        for i, name in enumerate(loads):
            copies[name] = pltpu.make_async_copy(r[name], r[name + "v"], r["sem"].at[i])
            copies[name].start()
        clear_edges(r["q"])
        copies["x"].wait()
        x = unpack(r["xv"])
        if tick == 4:
            x = x + x
        if tick >= 5:
            copies["skip"].wait()
            x = x + unpack(r["skipv"])
        copies["ones"].wait()
        ones = r["onesv"][...]
        za, ra = normed(x, ones)
        r["zav"][...] = za
        save_a = pltpu.make_async_copy(r["zav"], r["za"], r["sem"].at[8])
        save_a.start()
        put_shifted(r["q"], za * sigmoid(za))
        copies["w1"].wait()
        copies["bias"].wait()
        mid = conv(r["q"], r["w1v"]) + r["biasv"][0:1, :]
        zb, rb = normed(mid, ones)
        r["zbv"][...] = zb
        save_b = pltpu.make_async_copy(r["zbv"], r["zb"], r["sem"].at[9])
        save_b.start()
        r["scv"][...] = jnp.concatenate([ra, rb, jnp.zeros((6, CH), F32)], axis=0)
        save_c = pltpu.make_async_copy(r["scv"], r["sc"], r["sem"].at[10])
        save_c.start()
        put_shifted(r["q"], zb * sigmoid(zb))
        copies["w2"].wait()
        y = x + conv(r["q"], r["w2v"])
        if tick == 7:
            copies["target"].wait()
            y = (y - r["targetv"][...].astype(F32)) * (1.0 / math.sqrt(PIX))
        pack(r["yv"], y)
        out = pltpu.make_async_copy(r["yv"], r["y"], r["sem"].at[11])
        out.start()
        save_a.wait()
        save_b.wait()
        save_c.wait()
        out.wait()


def forward(tick, sec, x, w1, w2, bias, ones, skip, target, saved):
    args = [sec, x, w1, w2, bias, ones]
    if tick >= 5:
        args.append(skip)
    if tick == 7:
        args.append(target)
    aliases = {}
    if saved is not None:
        aliases = {len(args) + i: 1 + i for i in range(3)}
        args += list(saved)
    image = jax.ShapeDtypeStruct((PIX, CH), F32)
    outs = pl.pallas_call(
        functools.partial(fwd_kernel, tick, saved is not None),
        out_shape=(jax.ShapeDtypeStruct((PACK, 128), F32), image, image, jax.ShapeDtypeStruct((8, CH), F32)),
        in_specs=[SMEM] + [ANY] * (len(args) - 1),
        out_specs=(ANY,) * 4,
        scratch_shapes=[
            pltpu.VMEM((PACK, 128), F32),
            pltpu.VMEM((KROWS, CH), BF16),
            pltpu.VMEM((KROWS, CH), BF16),
            pltpu.VMEM((8, CH), F32),
            pltpu.VMEM((CH, CH), BF16),
            pltpu.VMEM((PACK, 128), F32),
            pltpu.VMEM((PIX, CH), BF16),
            pltpu.VMEM((PIX + 2 * WIDTH, 3 * CH), BF16),
            pltpu.VMEM((PIX, CH), F32),
            pltpu.VMEM((PIX, CH), F32),
            pltpu.VMEM((8, CH), F32),
            pltpu.VMEM((PACK, 128), F32),
            pltpu.SemaphoreType.DMA((12,)),
        ],
        input_output_aliases=aliases,
        compiler_params=pltpu.CompilerParams(vmem_limit_bytes=24 << 20),
        cost_estimate=pl.CostEstimate(flops=4 * PIX * KROWS * CH, bytes_accessed=5 << 20, transcendentals=2 * PIX * CH),
        name="section_fwd",
    )(*args)
    return outs[0], outs[1:]


def bwd_kernel(tick, aliased, *refs):
    names = ["sec", "g", "w1t", "w2t", "ones", "za", "zb", "sc"]
    if tick < 3:
        names.append("skip")
    if aliased:
        names += ["_gb", "_gm", "_db"]
    if tick > 0:
        names.append("gu")
    names += ["gb", "gm", "db"]
    names += ["gv", "skipv", "w1tv", "w2tv", "onesv", "zav", "zbv", "scv", "q", "gbv", "gmv", "dbv", "guv", "sem"]
    r = dict(zip(names, refs, strict=True))

    @pl.when(r["sec"][0] == tick)
    def _():
        copies = {}
        loads = ["g", "w2t", "zb", "sc", "ones"]
        if tick < 3:
            loads.insert(1, "skip")
        if tick > 0:
            loads += ["w1t", "za"]
        for i, name in enumerate(loads):
            copies[name] = pltpu.make_async_copy(r[name], r[name + "v"], r["sem"].at[i])
            copies[name].start()
        clear_edges(r["q"])
        copies["g"].wait()
        g = unpack(r["gv"])
        if tick == 3:
            g = g + g
        if tick < 3:
            copies["skip"].wait()
            g = g + unpack(r["skipv"])
        r["gbv"][...] = g.astype(BF16)
        save_g = pltpu.make_async_copy(r["gbv"], r["gb"], r["sem"].at[8])
        save_g.start()
        put_shifted(r["q"], g)
        copies["w2t"].wait()
        cot = conv(r["q"], r["w2tv"])
        copies["zb"].wait()
        copies["sc"].wait()
        copies["ones"].wait()
        ones = r["onesv"][...]
        gm = norm_back(r["zbv"][...], r["scv"][1:2, :], cot, ones)
        r["gmv"][...] = gm.astype(BF16)
        save_m = pltpu.make_async_copy(r["gmv"], r["gm"], r["sem"].at[9])
        save_m.start()
        r["dbv"][...] = jnp.concatenate([colsum(gm), jnp.zeros((7, CH), F32)], axis=0)
        save_b = pltpu.make_async_copy(r["dbv"], r["db"], r["sem"].at[10])
        save_b.start()
        if tick > 0:
            put_shifted(r["q"], gm)
            copies["w1t"].wait()
            cot = conv(r["q"], r["w1tv"])
            copies["za"].wait()
            gu = g + norm_back(r["zav"][...], r["scv"][0:1, :], cot, ones)
            pack(r["guv"], gu)
            out = pltpu.make_async_copy(r["guv"], r["gu"], r["sem"].at[11])
            out.start()
            out.wait()
        save_g.wait()
        save_m.wait()
        save_b.wait()


def backward(tick, sec, g, w1t, w2t, ones, kept, skip, saved):
    args = [sec, g, w1t, w2t, ones, *kept]
    if tick < 3:
        args.append(skip)
    first = 1 if tick > 0 else 0
    aliases = {}
    if saved is not None:
        aliases = {len(args) + i: first + i for i in range(3)}
        args += list(saved)
    low = jax.ShapeDtypeStruct((PIX, CH), BF16)
    out_shape = (low, low, jax.ShapeDtypeStruct((8, CH), F32))
    if tick > 0:
        out_shape = (jax.ShapeDtypeStruct((PACK, 128), F32),) + out_shape
    outs = pl.pallas_call(
        functools.partial(bwd_kernel, tick, saved is not None),
        out_shape=out_shape,
        in_specs=[SMEM] + [ANY] * (len(args) - 1),
        out_specs=(ANY,) * len(out_shape),
        scratch_shapes=[
            pltpu.VMEM((PACK, 128), F32),
            pltpu.VMEM((PACK, 128), F32),
            pltpu.VMEM((KROWS, CH), BF16),
            pltpu.VMEM((KROWS, CH), BF16),
            pltpu.VMEM((CH, CH), BF16),
            pltpu.VMEM((PIX, CH), F32),
            pltpu.VMEM((PIX, CH), F32),
            pltpu.VMEM((8, CH), F32),
            pltpu.VMEM((PIX + 2 * WIDTH, 3 * CH), BF16),
            pltpu.VMEM((PIX, CH), BF16),
            pltpu.VMEM((PIX, CH), BF16),
            pltpu.VMEM((8, CH), F32),
            pltpu.VMEM((PACK, 128), F32),
            pltpu.SemaphoreType.DMA((12,)),
        ],
        input_output_aliases=aliases,
        compiler_params=pltpu.CompilerParams(vmem_limit_bytes=24 << 20),
        cost_estimate=pl.CostEstimate(flops=4 * PIX * KROWS * CH, bytes_accessed=5 << 20, transcendentals=2 * PIX * CH),
        name="section_bwd",
    )(*args)
    return (outs[0] if tick > 0 else None), outs[first:]


def grad_kernel(part_of_time, z0, z1, g0, g1, time, out, q, gt, whole):
    for i, (z, g) in enumerate(((z0, g0), (z1, g1))):
        clear_edges(q.at[i])
        value = z[...]
        put_shifted(q.at[i], value * sigmoid(value))
        gt[i] = jnp.transpose(g[...].astype(F32)).astype(BF16)
    for r in range(3):
        part = jnp.dot(gt[0], q[0, WIDTH * r : WIDTH * r + PIX, :], preferred_element_type=F32)
        part += jnp.dot(gt[1], q[1, WIDTH * r : WIDTH * r + PIX, :], preferred_element_type=F32)
        whole[:, 3 * CH * r : 3 * CH * (r + 1)] = part
    for k in range(22):
        out[CH * k : CH * (k + 1), :] = whole[:, 128 * k : 128 * (k + 1)]
    half = CH // 2
    out[22 * CH : GROWS, :] = jnp.concatenate([whole[:half, 2816:2880], whole[half:, 2816:2880]], axis=1)
    if part_of_time == 0:
        out[GROWS : GROWS + TE, :] = time[:, 0:128]
        out[GROWS + TE :, :] = jnp.concatenate([time[:half, 256:320], time[half:, 256:320]], axis=1)
    else:
        out[GROWS : GROWS + TE, :] = time[:, 128:256]
        out[GROWS + TE :, :] = jnp.zeros((half, 128), F32)


def weight_grad(part_of_time, z0, z1, g0, g1, time):
    return pl.pallas_call(
        functools.partial(grad_kernel, part_of_time),
        out_shape=jax.ShapeDtypeStruct((2 * HALF, 128), F32),
        scratch_shapes=[
            pltpu.VMEM((2, PIX + 2 * WIDTH, 3 * CH), BF16),
            pltpu.VMEM((2, CH, PIX), BF16),
            pltpu.VMEM((CH, KROWS), F32),
        ],
        compiler_params=pltpu.CompilerParams(vmem_limit_bytes=24 << 20),
        cost_estimate=pl.CostEstimate(flops=4 * PIX * KROWS * CH, bytes_accessed=5 << 20, transcendentals=2 * PIX * CH),
        name="weight_grad",
    )(z0, z1, g0, g1, time)


def unpack_kernel(core, mine, other, out):
    def write(low, high):
        for k in range(12):
            out[0, :, 128 * k : 128 * (k + 1)] = low[CH * k : CH * (k + 1), :]
        for k in range(10):
            out[0, :, 1536 + 128 * k : 1536 + 128 * (k + 1)] = high[CH * k : CH * (k + 1), :]
        tail = high[10 * CH : 10 * CH + CH // 2, :]
        out[0, :, 2816:2880] = jnp.concatenate([tail[:, :64], tail[:, 64:]], axis=0)

    @pl.when(core[0] == 0)
    def _():
        write(mine, other)

    @pl.when(core[0] == 1)
    def _():
        write(other, mine)


def unpack_grad(core, mine, other):
    vmem = pl.BlockSpec(memory_space=pltpu.VMEM)
    turned_out = pl.pallas_call(
        unpack_kernel,
        out_shape=jax.ShapeDtypeStruct((1, CH, KROWS), F32),
        in_specs=[SMEM, vmem, vmem],
        out_specs=vmem,
        compiler_params=pltpu.CompilerParams(vmem_limit_bytes=24 << 20),
        name="unpack_grad",
    )(core, mine, other)
    return jnp.swapaxes(turned_out, 1, 2)


def embed_times(times):
    middle = TE // 2
    freqs = jnp.exp(-math.log(10000.0) * jnp.arange(middle, dtype=F32) / middle)
    angles = times.astype(F32)[:, None] * freqs[None, :]
    return jnp.concatenate([jnp.cos(angles), jnp.sin(angles)], axis=1)


def packed_image(image):
    half = PIX // 2
    tail = jnp.concatenate([image[:half, 256:320], image[half:, 256:320]], axis=1)
    return jnp.concatenate([image[:, 0:128], image[:, 128:256], tail], axis=0)


def turned(weight):
    taps = weight.reshape(9, CH, CH)[::-1]
    return jnp.transpose(taps, (0, 2, 1)).reshape(KROWS, CH)


def along_z(value, sign):
    pairs = []
    for z in range(8):
        pairs += [(2 * z, 2 * ((z + sign) % 8)), (2 * z + 1, 2 * ((z - sign) % 8) + 1)]
    return lax.ppermute(value, ("z", "core"), pairs)


def reduced(streams):
    core, z = lax.axis_index("core"), lax.axis_index("z")
    way = 1 - 2 * core
    swap = [(0, 1), (1, 0)]

    def chunk(blocks, ahead):
        return lax.dynamic_index_in_dim(blocks, (z + way * ahead + 8) % 8, 0, keepdims=False)

    mine = []
    for packed in streams:
        halves = packed.reshape(2, HALF, 128)
        given = lax.dynamic_index_in_dim(halves, 1 - core, 0, keepdims=False)
        kept = lax.dynamic_index_in_dim(halves, core, 0, keepdims=False)
        mine.append((kept + lax.ppermute(given, "core", swap)).reshape(8, HALF // 8, 128))
    forth = [chunk(blocks, 4) for blocks in mine]
    back = [chunk(blocks, -3) for blocks in mine]
    for step in range(1, 5):
        for i, blocks in enumerate(mine):
            forth[i] = along_z(forth[i], 1)
            if step < 4:
                forth[i] = forth[i] + chunk(blocks, 4 - step)
                back[i] = along_z(back[i], -1)
            if step < 3:
                back[i] = back[i] + chunk(blocks, step - 3)
    total = []
    for i, blocks in enumerate(mine):
        part = forth[i] + back[i] + chunk(blocks, 0)
        total.append(part + lax.ppermute(part, "x_hi", swap))
    whole = [lax.dynamic_update_index_in_dim(jnp.zeros_like(blocks), part, z, 0) for blocks, part in zip(mine, total)]
    forth, back = list(total), list(total)
    for step in range(1, 5):
        for i in range(len(total)):
            forth[i] = along_z(forth[i], 1)
            whole[i] = lax.dynamic_update_index_in_dim(whole[i], forth[i], (z - way * step + 8) % 8, 0)
            if step < 4:
                back[i] = along_z(back[i], -1)
                whole[i] = lax.dynamic_update_index_in_dim(whole[i], back[i], (z + way * step + 8) % 8, 0)
    result = []
    for blocks in whole:
        flat = blocks.reshape(HALF, 128)
        result.append((flat, lax.ppermute(flat, "core", swap)))
    return result


def crossed(sec, sent_by, arrived, pairs):
    sent_by = lax.optimization_barrier((sent_by, tuple(arrived)))[0]
    ticks = sorted(sent_by)
    moved = []
    for m in range(MICRO):
        value = sent_by[ticks[0]][m]
        for tick in ticks[1:]:
            value = jnp.where(sec[0] == tick, sent_by[tick][m], value)
        moved.append(lax.ppermute(value, "section", pairs))
    return moved


def local(features, target, timesteps, conv_one, conv_two, time_proj):
    sec = jnp.full((1,), lax.axis_index("section"), jnp.int32)
    w1, w2 = conv_one[0], conv_two[0]
    lanes = jnp.arange(CH) // (CH // GROUPS)
    ones = (lanes[:, None] == lanes[None, :]).astype(BF16)
    embedded = embed_times(timesteps)
    bias = jnp.dot(embedded, time_proj[0], precision=lax.Precision.HIGHEST)
    bias = jnp.broadcast_to(bias[:, None, :], (MICRO, 8, CH))
    images = features.reshape(MICRO, PIX, CH).astype(F32)
    targets = target.reshape(MICRO, PIX, CH)

    arrived = [packed_image(images[m]) for m in range(MICRO)]
    kept = [None] * MICRO
    sent_by = {}
    skips = None
    for tick in range(8):
        sent = [None] * MICRO
        for m in range(MICRO):
            skip = skips[m] if tick >= 5 else None
            sent[m], kept[m] = forward(tick, sec, arrived[m], w1, w2, bias[m], ones, skip, targets[m], kept[m])
            if tick < 7:
                arrived[m] = lax.ppermute(sent[m], "section", [(tick, tick + 1)])
        if tick == 0:
            w1t, w2t, _ = lax.optimization_barrier((w1, w2, sent[0]))
            w1t, w2t = turned(w1t), turned(w2t)
        if tick < 3:
            sent_by[tick] = tuple(sent)
        if tick == 2:
            skips = crossed(sec, sent_by, arrived, [(0, 7), (1, 6), (2, 5)])

    arrived = sent
    saved = [None] * MICRO
    sent_by = {}
    for tick in range(7, -1, -1):
        sent = [None] * MICRO
        for m in range(MICRO):
            skip = skips[m] if tick < 3 else None
            sent[m], saved[m] = backward(tick, sec, arrived[m], w1t, w2t, ones, kept[m], skip, saved[m])
            if tick > 0:
                arrived[m] = lax.ppermute(sent[m], "section", [(tick, tick - 1)])
        if tick > 4:
            sent_by[tick] = tuple(sent)
        if tick == 5:
            skips = crossed(sec, sent_by, arrived, [(7, 0), (6, 1), (5, 2)])

    grad_bias = jnp.concatenate([saved[m][2][0:1] for m in range(MICRO)], axis=0)
    grad_time = jnp.dot(embedded.T, grad_bias, precision=lax.Precision.HIGHEST)
    grad_two = weight_grad(1, kept[0][1], kept[1][1], saved[0][0], saved[1][0], grad_time)
    grad_one = weight_grad(0, kept[0][0], kept[1][0], saved[0][1], saved[1][1], grad_time)
    (two, one) = reduced([grad_two, grad_one])
    core = jnp.full((1,), lax.axis_index("core"), jnp.int32)
    ends = [jnp.where(core[0] == 0, other[GROWS - HALF :], mine[GROWS - HALF :]) for mine, other in (one, two)]
    tail = ends[0][TE:]
    last = jnp.concatenate([tail[:, :64], tail[:, 64:]], axis=0)
    sum_time = jnp.concatenate([ends[0][:TE], ends[1][:TE], last], axis=1)
    return unpack_grad(core, *one), unpack_grad(core, *two), sum_time[None]


def solution(mesh):
    inner = Mesh(mesh.devices.reshape(2, 8, 2, 8), ("x_hi", "z", "core", "section"))
    batch = ("x_hi", "z", "core")
    by_section = P("section", None, None)
    return jax.shard_map(
        local,
        mesh=inner,
        in_specs=(P(batch, None, None), P(batch, None, None), P(batch), by_section, by_section, by_section),
        out_specs=(by_section, by_section, by_section),
        check_vma=False,
    )
```
